128 devices in a mesh: gx: 8 (over x, y_hi), gy: 16 (over y_lo, z, core).
Axes of the slice: x: 4, y: 4 (y_hi: 2, y_lo: 2; y = y_hi * 2 + y_lo), z: 4, core: 2. Of those that a mesh axis runs over, the one named last changes fastest.
Arguments:
- probes: bfloat16 [16, 64, 64, 384], P('gx', 'gy'), may hold values from -6 to 6
- counts: int32 [16, 64], P('gx', 'gy'), may hold values from 1 to 128, 3276 in all within a row
- blocks: bfloat16 [16, 64, 9, 384, 384], P('gx', 'gy'), as said below
Outputs:
- displacements: bfloat16 [16, 64, 64, 384], P('gx', 'gy')
- msd: float32 [16, 64, 384], P('gx', 'gy')
The draws below stay inside these ranges and needn't reach their ends.
Inputs may be any that keep to these rules, and one draw needn't show every extreme that they name: Each row counts[x, :] sums to 3276, and its largest entry is 128. blocks[a, 3 (dx + 1) + (dy + 1)] is the transpose of blocks[a + (dx, dy), 3 (1 - dx) + (1 - dy)] (cells taken periodically), so blocks[a, 4] is symmetric.
All inputs are finite; a program needn't handle non-finite values. No bound on the sum of `counts` on one device may be relied on, other than what follows from the above.
Results may differ from the reference program's by a relative error of at most 0.006.
Values may be sent and summed in bfloat16 or wider, within the bound.
No kernel may reach another device: no remote copies, remote signals or barrier semaphores. Data moves between devices by JAX's collectives and lax.ppermute only.
A program may use at most 64 MiB of HBM per device.

```python
import math
import jax
import jax.numpy as jnp
import numpy as np
from jax import lax

SLOTS = 128
DOFS = 384
PROBES = 64
TERMS = 8
NXC = 16
NYC = 64


def draw_blocks(key, part):
    scale = (32.0 * DOFS) ** (-0.5)
    shape = (NXC, NYC, 4, DOFS, DOFS)
    self_shape = (NXC, NYC, DOFS, DOFS)
    forward = jax.random.normal(key, shape, jnp.float32) * scale
    middle = jax.random.normal(jax.random.fold_in(key, 7), self_shape, jnp.float32) * scale
    middle = (middle + jnp.swapaxes(middle, 2, 3)) * 0.70710678
    forward = forward.astype(jnp.bfloat16)
    middle = middle.astype(jnp.bfloat16)
    down_up = forward[:, :, 0]
    down_mid = forward[:, :, 1]
    down_down = forward[:, :, 2]
    mid_up = forward[:, :, 3]

    def reverse(block, shift_x, shift_y):
        return jnp.swapaxes(jnp.roll(block, (shift_x, shift_y), axis=(0, 1)), 2, 3)
    pieces = [reverse(down_down, 1, 1), reverse(down_mid, 1, 0), reverse(down_up, 1, -1), reverse(mid_up, 0, 1), middle, mid_up, down_up, down_mid, down_down]
    return jnp.stack(pieces, axis=2)


def steps_of(key, shape, split, smallest, largest):
    factor_of, own = 1.0, jax.random.fold_in(key, 6)
    for dim, parts in split:
        draws = jnp.exp(jax.random.uniform(jax.random.fold_in(own, dim), (parts,), jnp.float32, smallest / len(split), largest / len(split)))
        factor_of = factor_of * jnp.repeat(draws, shape[dim] // parts).reshape([-1 if axis == dim else 1 for axis in range(len(shape))])
    return factor_of


def profile(count, total, bound, slope):
    weights = [(1 << 20) // math.isqrt(grade ** slope) + 1 for grade in range(2, count + 1)]
    surplus, given = total - bound - (count - 1), [1] * (count - 1)
    while surplus > 0:
        candidates = [i for i in range(count - 1) if given[i] < bound]
        whole, left = sum([weights[i] for i in candidates]), surplus
        for i in candidates:
            addition = min(bound - given[i], max(1, left * weights[i] // whole), surplus)
            given[i] = given[i] + addition
            surplus = surplus - addition
    return np.array([bound] + given)


def uneven_parts(own_key, amount, total, bound, slope):
    if amount == 2:
        one = jax.random.randint(own_key, (), max(1, total - bound), min(bound, total - 1) + 1)
        return jnp.stack([one, total - one])
    tallies = jnp.asarray(profile(amount, total, bound, slope), jnp.int32)
    couples = (amount - 1) // 2
    source_of, sink = tallies[1:1 + 2 * couples:2], tallies[2:2 + 2 * couples:2]
    slack = jnp.minimum(source_of - 1, bound - sink)
    moved = jax.random.randint(jax.random.fold_in(own_key, 1), (couples,), 0, 1 << 20) % (slack + 1)
    tallies = tallies.at[1:1 + 2 * couples:2].set(source_of - moved).at[2:2 + 2 * couples:2].set(sink + moved)
    return tallies[jax.random.permutation(jax.random.fold_in(own_key, 2), amount)]


def gaussian(key, shape, width, most, split=(), kind=jnp.bfloat16):
    values = jax.random.normal(key, shape, jnp.float32) * width
    if len(split) > 0:
        values = steps_of(key, shape, split, -0.22, 0.18) * values
    return jnp.clip(values, min=-most, max=most).astype(kind)


def setup_inputs(seed: int = 0) -> dict:
    arg_keys = jax.random.split(jax.random.key(seed), 4)
    return {
        "probes": gaussian(arg_keys[0], (NXC, NYC, PROBES, DOFS), 1.0, 6.0, ((0, 8), (1, 16))),
        "counts": jax.vmap(lambda own: uneven_parts(own, NYC, 2 * NYC * SLOTS // 5, SLOTS, 2))(jax.random.split(arg_keys[1], NXC)).reshape((NXC, NYC)).astype(jnp.int32),
        "blocks": draw_blocks(jax.random.fold_in(arg_keys[3], 71), 0),
    }


inverse_temp = 4.0
low_band = 0.02
high_band = 1.0

def chebyshev_weights(term_count):
    node_count = 64
    values = []
    angles = []
    for n in range(node_count):
        angle = math.pi * (n + 0.5) / node_count
        energy = low_band + (math.cos(angle) + 1.0) * (high_band - low_band) / 2.0
        root_energy = math.sqrt(energy)
        decay = math.exp(-inverse_temp * root_energy)
        values.append((1.0 + decay) / (1.0 - decay) / (2.0 * root_energy))
        angles.append(angle)
    coeffs = []
    for k in range(term_count):
        total = 0.0
        for n in range(node_count):
            total = total + values[n] * math.cos(k * angles[n])
        coeffs.append(2.0 / node_count * total)
    coeffs[0] = coeffs[0] / 2.0
    return [float(np.float32(c)) for c in coeffs]

def apply_operator(source, blocks, live_mask):
    rounded = source.astype(jnp.bfloat16)
    moved = []
    for shift_x in (-1, 0, 1):
        for shift_y in (-1, 0, 1):
            moved.append(jnp.roll(rounded, (-shift_x, -shift_y), axis=(0, 1)))
    stacked = jnp.stack(moved, axis=2)

    def row_apply(pair):
        nearby, block_row = pair
        return jnp.einsum('ykpj,ykij->ypi', nearby.astype(jnp.float32), block_row.astype(jnp.float32))
    result = lax.map(row_apply, (stacked, blocks))
    return result * live_mask[:, :, None, :]

def reference(probes, counts, blocks):
    coeffs = chebyshev_weights(TERMS)
    atom_index = jnp.arange(DOFS).astype(jnp.int32) // 3
    live_mask = (atom_index[None, None, :] < counts[:, :, None]).astype(jnp.float32)
    start_term = probes.astype(jnp.float32) * live_mask[:, :, None, :]
    previous = start_term
    current = apply_operator(start_term, blocks, live_mask)
    summed = coeffs[0] * start_term + coeffs[1] * current
    for k in range(2, TERMS):
        following = 2.0 * apply_operator(current, blocks, live_mask) - previous
        summed = summed + coeffs[k] * following
        previous, current = (current, following)
    displacements = summed.astype(jnp.bfloat16)
    msd = lax.optimization_barrier(jnp.mean(start_term * summed, axis=2))
    return (displacements, msd)
```

```python
import math

import jax
import jax.numpy as jnp
import numpy as np
from jax import lax
from jax.experimental import pallas as pl
from jax.experimental.pallas import tpu as pltpu
from jax.sharding import PartitionSpec as P

TERMS = 8


inverse_temp = 4.0
low_band = 0.02
high_band = 1.0

ROWS = 2
COLS = 4
FORWARD = (((1,), (1,)), ((), ()))


def chebyshev_weights(term_count):
    node_count = 64
    values = []
    angles = []
    for n in range(node_count):
        angle = math.pi * (n + 0.5) / node_count
        energy = low_band + (math.cos(angle) + 1.0) * (high_band - low_band) / 2.0
        root_energy = math.sqrt(energy)
        decay = math.exp(-inverse_temp * root_energy)
        values.append((1.0 + decay) / (1.0 - decay) / (2.0 * root_energy))
        angles.append(angle)
    coeffs = []
    for k in range(term_count):
        total = 0.0
        for n in range(node_count):
            total = total + values[n] * math.cos(k * angles[n])
        coeffs.append(2.0 / node_count * total)
    coeffs[0] = coeffs[0] / 2.0
    return [float(np.float32(c)) for c in coeffs]


def place(parity, row, col):
    odd_x = parity[0]
    odd_y = parity[1]
    x = odd_x if row == 0 else 1 - odd_x
    y = (3 - col) + odd_y * (2 * col - 3)
    return x, y


def toward(parity, step_row, step_col):
    odd_x = parity[0]
    odd_y = parity[1]
    dx = (2 * odd_x, 1, 2 - 2 * odd_x)[step_row]
    dy = (2 - 2 * odd_y, 1, 2 * odd_y)[step_col]
    return 3 * dx + dy


def start_kernel(parity, counts, probes, far, near):
    lane = lax.broadcasted_iota(jnp.int32, probes.shape[2:], 1)
    for row, out in enumerate((far, near)):
        for col in range(COLS):
            x, y = place(parity, row, col)
            live = lane < 3 * counts[x, y]
            out[col] = jnp.where(live, probes[x, y].astype(jnp.float32), 0.0).astype(jnp.bfloat16)


def load_kernel(parity, blocks, out, sems):
    copies = []
    for row in range(ROWS):
        for col in range(COLS):
            x, y = place(parity, row, col)
            for step_row in range(3):
                for step_col in range(3):
                    slot = 3 * step_row + step_col
                    copies.append(
                        pltpu.make_async_copy(
                            blocks.at[x, y, toward(parity, step_row, step_col)],
                            out.at[row, col, slot],
                            sems.at[9 * (4 * row + col) + slot],
                        )
                    )
    for copy in copies:
        copy.start()
    for copy in copies:
        copy.wait()


def product(blocks, row, col, pieces):
    left = jnp.concatenate([blocks[row, col, slot] for slot, _ in pieces], axis=1)
    right = jnp.concatenate([v for _, v in pieces], axis=1)
    return lax.dot_general(left, right, FORWARD, preferred_element_type=jnp.float32)


def own_kernel(far, near, blocks, total):
    for row in range(ROWS):
        for col in range(COLS):
            pieces = []
            for other, ref in enumerate((far, near)):
                step_row = other - row + 1
                for step_col in range(3):
                    c = col + step_col - 1
                    if 0 <= c < COLS:
                        pieces.append((3 * step_row + step_col, ref[c]))
            total[row, col] = product(blocks, row, col, pieces)


def row_kernel(halo_far, halo_near, blocks, partial, total):
    for row, ref in enumerate((halo_far, halo_near)):
        for col in range(COLS):
            pieces = []
            for step_col in range(3):
                c = col + step_col - 1
                if 0 <= c < COLS:
                    pieces.append((3 * (2 * row) + step_col, ref[c]))
            total[row, col] = partial[row, col] + product(blocks, row, col, pieces)


def edge_kernel(halo_far, far, near, halo_near, core_edge, chip_edge):
    for slot, ref in enumerate((halo_far, far, near, halo_near)):
        core_edge[slot] = ref[0]
        chip_edge[slot] = ref[COLS - 1]


def column_sums(halo_core, halo_chip, blocks):
    sums = {}
    for col, step_col, ref in ((0, 0, halo_core), (3, 2, halo_chip)):
        for row in range(ROWS):
            pieces = [(3 * s + step_col, ref[row + s]) for s in range(3)]
            sums[row, col] = product(blocks, row, col, pieces)
    return sums


def step_kernel(index, coeffs, refs):
    refs = list(refs)
    parity, counts, halo_core, halo_chip, blocks, partial = refs[:6]
    rest = refs[6:]
    last = index == TERMS - 1
    if index == 1:
        start = rest[:2]
        rest = rest[2:]
    else:
        before, now, summed_in = rest[:3]
        rest = rest[3:]
        if last:
            start = rest[:2]
            rest = rest[2:]
    lane = lax.broadcasted_iota(jnp.int32, (64, 384), 1)
    sums = column_sums(halo_core, halo_chip, blocks)
    for row in range(ROWS):
        for col in (1, 2, 0, 3):
            x, y = place(parity, row, col)
            raw = partial[row, col]
            if (row, col) in sums:
                raw = raw + sums[row, col]
            applied = jnp.where(lane < 3 * counts[x, y], raw.T, 0.0)
            if index == 1:
                first = start[row][col].astype(jnp.float32)
                term = applied
                summed = coeffs[0] * first + coeffs[1] * term
            else:
                term = 2.0 * applied - before_of(before, row, col)
                summed = summed_in[row, col] + coeffs[index] * term
            if last:
                displacements, msd = rest
                displacements[x, y] = summed.astype(jnp.bfloat16)
                first = start[row][col].astype(jnp.float32)
                msd[x, y] = jnp.sum(first * summed, axis=0, keepdims=True) * (1.0 / 64.0)
            else:
                term_out, summed_out, far, near = rest
                term_out[row, col] = term
                summed_out[row, col] = summed
                (far, near)[row][col] = term.astype(jnp.bfloat16)


def before_of(before, row, col):
    if isinstance(before, tuple):
        return before[row][col].astype(jnp.float32)
    return before[row, col]


def local(probes, counts, blocks):
    coeffs = chebyshev_weights(TERMS)
    x_index = lax.axis_index("gx")
    y_index = lax.axis_index("gy")
    parity = jnp.stack([x_index % 2, y_index % 2]).astype(jnp.int32)
    vmem = pl.BlockSpec(memory_space=pltpu.VMEM)
    smem = pl.BlockSpec(memory_space=pltpu.SMEM)
    hbm = pl.BlockSpec(memory_space=pl.ANY)
    dofs = probes.shape[3]
    count = probes.shape[2]
    cells = (COLS, count, dofs)
    state = jax.ShapeDtypeStruct((ROWS, COLS, count, dofs), jnp.float32)
    raw = jax.ShapeDtypeStruct((ROWS, COLS, dofs, count), jnp.float32)
    rounded = jax.ShapeDtypeStruct(cells, jnp.bfloat16)
    params = pltpu.CompilerParams(vmem_limit_bytes=16 * 1024 * 1024)

    def cost(pairs):
        flops = 2 * pairs * count * dofs * dofs * 4
        return pl.CostEstimate(flops=flops, bytes_accessed=pairs * dofs * dofs * 2, transcendentals=0)

    def swap(value, axis, far):
        size = lax.axis_size(axis)
        if far:
            pairs = [(i, (i + 1) % size if i % 2 else (i - 1) % size) for i in range(size)]
        else:
            pairs = [(i, i ^ 1) for i in range(size)]
        return lax.ppermute(value, axis, pairs)

    far, near = pl.pallas_call(
        start_kernel,
        out_shape=(rounded, rounded),
        in_specs=[smem, smem, vmem],
        out_specs=(vmem, vmem),
        compiler_params=params,
        name="start",
    )(parity, counts, probes)
    start = (far, near)
    held = pl.pallas_call(
        load_kernel,
        out_shape=pltpu.VMEM(blocks.shape, blocks.dtype),
        in_specs=[smem, hbm],
        out_specs=vmem,
        scratch_shapes=[pltpu.SemaphoreType.DMA((72,))],
        compiler_params=params,
        cost_estimate=pl.CostEstimate(flops=0, bytes_accessed=blocks.size * 4, transcendentals=0),
        name="load",
    )(parity, blocks)

    before = now = summed = None
    for index in range(1, TERMS):
        halo_far = swap(far, "gx", True)
        halo_near = swap(near, "gx", False)
        partial = pl.pallas_call(
            own_kernel,
            out_shape=raw,
            in_specs=[vmem, vmem, vmem],
            out_specs=vmem,
            compiler_params=params,
            cost_estimate=cost(40),
            name="own",
        )(far, near, held)
        halo_far, halo_near, partial = lax.optimization_barrier((halo_far, halo_near, partial))
        core_edge, chip_edge = pl.pallas_call(
            edge_kernel,
            out_shape=(rounded, rounded),
            in_specs=[vmem] * 4,
            out_specs=(vmem, vmem),
            compiler_params=params,
            name="edges",
        )(halo_far, far, near, halo_near)
        halo_core = swap(core_edge, "gy", False)
        halo_chip = swap(chip_edge, "gy", True)
        partial = pl.pallas_call(
            row_kernel,
            out_shape=raw,
            in_specs=[vmem] * 4,
            out_specs=vmem,
            compiler_params=params,
            cost_estimate=cost(20),
            name="rows",
        )(halo_far, halo_near, held, partial)
        last = index == TERMS - 1
        operands = [parity, counts, halo_core, halo_chip, held, partial]
        if index == 1:
            operands += list(start)
        else:
            operands += ([*start] if index == 2 else [before]) + [summed]
            if last:
                operands += list(start)
        if last:
            outs = (
                jax.ShapeDtypeStruct(probes.shape, jnp.bfloat16),
                jax.ShapeDtypeStruct((ROWS, COLS, 1, dofs), jnp.float32),
            )
        else:
            outs = (state, state, rounded, rounded)

        def body(*refs, index=index, last=last):
            fixed = list(refs[:6])
            tail = list(refs[6:])
            if index == 2:
                fixed += [tuple(tail[:2]), None, tail[2]]
                tail = tail[3:]
            elif index > 2:
                fixed += [tail[0], None, tail[1]]
                tail = tail[2:]
            step_kernel(index, coeffs, fixed + tail)

        results = pl.pallas_call(
            body,
            out_shape=outs,
            in_specs=[smem, smem] + [vmem] * (len(operands) - 2),
            out_specs=tuple([vmem] * len(outs)),
            compiler_params=params,
            cost_estimate=cost(12),
            name="step",
        )(*operands)
        if last:
            displacements, msd = results
        else:
            before, now = now, results[0]
            summed, far, near = results[1:]
    return displacements, msd.reshape(ROWS, COLS, dofs)


def solution(mesh):
    return jax.shard_map(
        local,
        mesh=mesh,
        in_specs=(P("gx", "gy", None, None), P("gx", "gy"), P("gx", "gy", None, None, None)),
        out_specs=(P("gx", "gy", None, None), P("gx", "gy", None)),
        check_vma=False,
    )
```

```python
import math

import jax
import jax.numpy as jnp
import numpy as np
from jax import lax
from jax.experimental import pallas as pl
from jax.experimental.pallas import tpu as pltpu
from jax.sharding import PartitionSpec as P


TERMS = 8


inverse_temp = 4.0
low_band = 0.02
high_band = 1.0

ROWS = 2
COLS = 4
FORWARD = (((1,), (1,)), ((), ()))


def chebyshev_weights(term_count):
    node_count = 64
    values = []
    angles = []
    for n in range(node_count):
        angle = math.pi * (n + 0.5) / node_count
        energy = low_band + (math.cos(angle) + 1.0) * (high_band - low_band) / 2.0
        root_energy = math.sqrt(energy)
        decay = math.exp(-inverse_temp * root_energy)
        values.append((1.0 + decay) / (1.0 - decay) / (2.0 * root_energy))
        angles.append(angle)
    coeffs = []
    for k in range(term_count):
        total = 0.0
        for n in range(node_count):
            total = total + values[n] * math.cos(k * angles[n])
        coeffs.append(2.0 / node_count * total)
    coeffs[0] = coeffs[0] / 2.0
    return [float(np.float32(c)) for c in coeffs]


def place(parity, row, col):
    odd_x = parity[0]
    odd_y = parity[1]
    x = odd_x if row == 0 else 1 - odd_x
    y = (3 - col) + odd_y * (2 * col - 3)
    return x, y


def toward(parity, step_row, step_col):
    odd_x = parity[0]
    odd_y = parity[1]
    dx = (2 * odd_x, 1, 2 - 2 * odd_x)[step_row]
    dy = (2 - 2 * odd_y, 1, 2 * odd_y)[step_col]
    return 3 * dx + dy


def start_kernel(parity, counts, probes, far, near):
    lane = lax.broadcasted_iota(jnp.int32, probes.shape[2:], 1)
    for row, out in enumerate((far, near)):
        for col in range(COLS):
            x, y = place(parity, row, col)
            live = lane < 3 * counts[x, y]
            out[col] = jnp.where(live, probes[x, y].astype(jnp.float32), 0.0).astype(jnp.bfloat16)


def load_kernel(parity, blocks, far, near, out, total, sems):
    cells = [(row, col) for row in range(ROWS) for col in range(COLS)]
    for row, col in cells:
        x, y = place(parity, row, col)
        for step_row in range(3):
            for step_col in range(3):
                pltpu.make_async_copy(
                    blocks.at[x, y, toward(parity, step_row, step_col)],
                    out.at[row, col, 3 * step_row + step_col],
                    sems.at[COLS * row + col],
                ).start()
    for row, col in cells:
        pltpu.make_async_copy(blocks.at[row, col], out.at[row, col], sems.at[COLS * row + col]).wait()
        total[row, col] = own_product(far, near, out, row, col)


def product(blocks, row, col, pieces):
    left = jnp.concatenate([blocks[row, col, slot] for slot, _ in pieces], axis=1)
    right = jnp.concatenate([v for _, v in pieces], axis=1)
    return lax.dot_general(left, right, FORWARD, preferred_element_type=jnp.float32)


def own_product(far, near, blocks, row, col):
    pieces = []
    for other, ref in enumerate((far, near)):
        step_row = other - row + 1
        for step_col in range(3):
            c = col + step_col - 1
            if 0 <= c < COLS:
                pieces.append((3 * step_row + step_col, ref[c]))
    return product(blocks, row, col, pieces)


def own_kernel(far, near, blocks, total):
    for row in range(ROWS):
        for col in range(COLS):
            total[row, col] = own_product(far, near, blocks, row, col)


def row_product(ref, blocks, row, col):
    pieces = []
    for step_col in range(3):
        c = col + step_col - 1
        if 0 <= c < COLS:
            pieces.append((3 * (2 * row) + step_col, ref[c]))
    return product(blocks, row, col, pieces)


def column_product(ref, blocks, row, col):
    step_col = 0 if col == 0 else 2
    return product(blocks, row, col, [(3 * s + step_col, ref[row + s]) for s in range(3)])


def edge_kernel(halo_far, far, near, halo_near, core_edge, chip_edge):
    for slot, ref in enumerate((halo_far, far, near, halo_near)):
        core_edge[slot] = ref[0]
        chip_edge[slot] = ref[COLS - 1]


def advance(index, coeffs, parity, counts, state, cols, slot, row, raw):
    col = cols[slot]
    x, y = place(parity, row, col)
    lane = lax.broadcasted_iota(jnp.int32, raw.shape[::-1], 1)
    applied = jnp.where(lane < 3 * counts[x, y], raw.T, 0.0)
    first = None
    if index in (1, 2, TERMS - 1):
        first = state[-2:][row][col].astype(jnp.float32)
    if index == 1:
        return applied, coeffs[0] * first + coeffs[1] * applied, None
    if index == 2:
        summed, before = state[0][row, slot], first
    else:
        summed, before = state[0][row, slot], state[1][row, slot]
    term = 2.0 * applied - before
    summed = summed + coeffs[index] * term
    msd = None
    if index == TERMS - 1:
        msd = jnp.sum(first * summed, axis=0, keepdims=True) * (1.0 / raw.shape[1])
    return term, summed, msd


def state_size(index):
    return {1: 2, 2: 3, TERMS - 1: 4}.get(index, 2)


def make_rows(index, coeffs):
    def rows(parity, counts, halo_far, halo_near, blocks, partial, *refs):
        state, outs = refs[: state_size(index)], refs[state_size(index) :]
        for row, ref in enumerate((halo_far, halo_near)):
            for col in (1, 2, 0, 3):
                raw = partial[row, col] + row_product(ref, blocks, row, col)
                if col in (0, 3):
                    outs[0 if col == 0 else 1][row] = raw
                    continue
                slot = col - 1
                term, summed, msd = advance(index, coeffs, parity, counts, state, (1, 2), slot, row, raw)
                if index == TERMS - 1:
                    outs[2][row, slot] = summed.astype(jnp.bfloat16)
                    outs[3][row, slot] = msd
                else:
                    outs[2][row, slot] = term.astype(jnp.bfloat16)
                    outs[3][row, slot] = summed
                    outs[4][row, slot] = term

    return rows


def make_core(index, coeffs):
    def core(parity, counts, halo, blocks, partial, *refs):
        state, outs = refs[: state_size(index)], refs[state_size(index) :]
        for row in range(ROWS):
            raw = partial[row] + column_product(halo, blocks, row, 0)
            term, summed, msd = advance(index, coeffs, parity, counts, state, (0,), 0, row, raw)
            if index == TERMS - 1:
                outs[0][row, 0] = summed.astype(jnp.bfloat16)
                outs[1][row, 0] = msd
            else:
                outs[0][row, 0] = term.astype(jnp.bfloat16)
                outs[1][row, 0] = summed
                outs[2][row, 0] = term

    return core


def make_chip(index, coeffs):
    last = index == TERMS - 1

    def chip(parity, counts, halo, blocks, partial, inner, core, *refs):
        if last:
            inner_msd, core_msd = refs[:2]
            refs = refs[2:]
        state, outs = refs[: state_size(index)], refs[state_size(index) :]
        for row in range(ROWS):
            raw = partial[row] + column_product(halo, blocks, row, 3)
            term, summed, msd = advance(index, coeffs, parity, counts, state, (3,), 0, row, raw)
            if not last:
                message = outs[row]
                message[0] = core[row, 0]
                message[1] = inner[row, 0]
                message[2] = inner[row, 1]
                message[3] = term.astype(jnp.bfloat16)
                outs[2][row, 0] = summed
                outs[3][row, 0] = term
                continue
            displacements, msd_out = outs
            pieces = [core[row, 0], inner[row, 0], inner[row, 1], summed.astype(jnp.bfloat16)]
            means = [core_msd[row, 0], inner_msd[row, 0], inner_msd[row, 1], msd]
            for col in range(COLS):
                x, y = place(parity, row, col)
                displacements[x, y] = pieces[col]
            x, _ = place(parity, row, 0)
            msd_out[x] = jnp.where(
                parity[1] == 1, jnp.concatenate(means, axis=0), jnp.concatenate(means[::-1], axis=0)
            )

    return chip


def local(probes, counts, blocks):
    coeffs = chebyshev_weights(TERMS)
    x_index = lax.axis_index("gx")
    y_index = lax.axis_index("gy")
    parity = jnp.stack([x_index % 2, y_index % 2]).astype(jnp.int32)
    vmem = pl.BlockSpec(memory_space=pltpu.VMEM)
    smem = pl.BlockSpec(memory_space=pltpu.SMEM)
    hbm = pl.BlockSpec(memory_space=pl.ANY)
    dofs = probes.shape[3]
    count = probes.shape[2]
    cells = (COLS, count, dofs)
    raw = jax.ShapeDtypeStruct((ROWS, COLS, dofs, count), jnp.float32)
    rounded = jax.ShapeDtypeStruct(cells, jnp.bfloat16)
    params = pltpu.CompilerParams(vmem_limit_bytes=16 * 1024 * 1024)

    def cost(pairs):
        flops = 2 * pairs * count * dofs * dofs * 4
        return pl.CostEstimate(flops=flops, bytes_accessed=pairs * dofs * dofs * 2, transcendentals=0)

    def swap(value, axis, far):
        size = lax.axis_size(axis)
        if far:
            pairs = [(i, (i + 1) % size if i % 2 else (i - 1) % size) for i in range(size)]
        else:
            pairs = [(i, i ^ 1) for i in range(size)]
        return lax.ppermute(value, axis, pairs)

    far, near = pl.pallas_call(
        start_kernel,
        out_shape=(rounded, rounded),
        in_specs=[smem, smem, vmem],
        out_specs=(vmem, vmem),
        compiler_params=params,
        name="start",
    )(parity, counts, probes)
    start = [far, near]

    def column_state(cols, dtype):
        return jax.ShapeDtypeStruct((ROWS, cols, count, dofs), dtype)

    def run(body, operands, outs, pairs):
        return pl.pallas_call(
            body,
            out_shape=outs,
            in_specs=[smem, smem] + [vmem] * (len(operands) - 2),
            out_specs=tuple([vmem] * len(outs)),
            compiler_params=params,
            cost_estimate=cost(pairs),
        )(*operands)

    edge = jax.ShapeDtypeStruct((ROWS, dofs, count), jnp.float32)
    saved = {"inner": [], "core": [], "chip": []}
    held = None
    for index in range(1, TERMS):
        last = index == TERMS - 1
        halo_near = swap(near, "gx", False)
        halo_far = swap(far, "gx", True)
        if index == 1:
            held, partial = pl.pallas_call(
                load_kernel,
                out_shape=(pltpu.VMEM(blocks.shape, blocks.dtype), raw),
                in_specs=[smem, hbm, vmem, vmem],
                out_specs=(vmem, vmem),
                scratch_shapes=[pltpu.SemaphoreType.DMA((ROWS * COLS,))],
                compiler_params=params,
                cost_estimate=pl.CostEstimate(flops=0, bytes_accessed=blocks.size * 4, transcendentals=0),
                name="load",
            )(parity, blocks, far, near)
        else:
            partial = pl.pallas_call(
                own_kernel,
                out_shape=raw,
                in_specs=[vmem, vmem, vmem],
                out_specs=vmem,
                compiler_params=params,
                cost_estimate=cost(40),
                name="own",
            )(far, near, held)
        halo_far, halo_near, partial = lax.optimization_barrier((halo_far, halo_near, partial))
        core_edge, chip_edge = pl.pallas_call(
            edge_kernel,
            out_shape=(rounded, rounded),
            in_specs=[vmem] * 4,
            out_specs=(vmem, vmem),
            compiler_params=params,
            name="edges",
        )(halo_far, far, near, halo_near)
        halo_core = swap(core_edge, "gy", False)
        halo_chip = swap(chip_edge, "gy", True)

        def state(name, index=index, last=last):
            return saved[name] + (start if index <= 2 or last else [])

        def outputs(cols, last=last):
            if last:
                mean = jax.ShapeDtypeStruct((ROWS, cols, 1, dofs), jnp.float32)
                return (column_state(cols, jnp.bfloat16), mean)
            wide = column_state(cols, jnp.float32)
            return (column_state(cols, jnp.bfloat16), wide, wide)

        def keep(name, summed, term, index=index):
            terms[name].append(term)
            saved[name] = [summed] + ([terms[name][-2]] if index >= 2 else [])

        if index == 1:
            terms = {"inner": [], "core": [], "chip": []}
        fixed = [parity, counts]
        core_raw, chip_raw, inner, *rest = run(
            make_rows(index, coeffs),
            fixed + [halo_far, halo_near, held, partial] + state("inner"),
            (edge, edge) + outputs(2),
            20,
        )
        core, *core_rest = run(
            make_core(index, coeffs),
            fixed + [halo_core, held, core_raw] + state("core"),
            outputs(1),
            6,
        )
        operands = fixed + [halo_chip, held, chip_raw, inner, core]
        if last:
            operands += [rest[0], core_rest[0]]
            outs = (
                jax.ShapeDtypeStruct(probes.shape, jnp.bfloat16),
                jax.ShapeDtypeStruct((ROWS, COLS, dofs), jnp.float32),
            )
        else:
            wide = column_state(1, jnp.float32)
            outs = (rounded, rounded, wide, wide)
        results = run(make_chip(index, coeffs), operands + state("chip"), outs, 6)
        if not last:
            far, near = results[:2]
            keep("inner", *rest)
            keep("core", *core_rest)
            keep("chip", *results[2:])
    return tuple(results)


def solution(mesh):
    return jax.shard_map(
        local,
        mesh=mesh,
        in_specs=(P("gx", "gy", None, None), P("gx", "gy"), P("gx", "gy", None, None, None)),
        out_specs=(P("gx", "gy", None, None), P("gx", "gy", None)),
        check_vma=False,
    )
```

```python
import math

import jax
import jax.numpy as jnp
import numpy as np
from jax import lax
from jax.experimental import pallas as pl
from jax.experimental.pallas import tpu as pltpu
from jax.sharding import PartitionSpec as P


TERMS = 8


inverse_temp = 4.0
low_band = 0.02
high_band = 1.0

ROWS = 2
COLS = 4
FORWARD = (((1,), (1,)), ((), ()))


def chebyshev_weights(term_count):
    node_count = 64
    values = []
    angles = []
    for n in range(node_count):
        angle = math.pi * (n + 0.5) / node_count
        energy = low_band + (math.cos(angle) + 1.0) * (high_band - low_band) / 2.0
        root_energy = math.sqrt(energy)
        decay = math.exp(-inverse_temp * root_energy)
        values.append((1.0 + decay) / (1.0 - decay) / (2.0 * root_energy))
        angles.append(angle)
    coeffs = []
    for k in range(term_count):
        total = 0.0
        for n in range(node_count):
            total = total + values[n] * math.cos(k * angles[n])
        coeffs.append(2.0 / node_count * total)
    coeffs[0] = coeffs[0] / 2.0
    return [float(np.float32(c)) for c in coeffs]


def place(parity, row, col):
    odd_x = parity[0]
    odd_y = parity[1]
    x = odd_x if row == 0 else 1 - odd_x
    y = (3 - col) + odd_y * (2 * col - 3)
    return x, y


def toward(parity, step_row, step_col):
    odd_x = parity[0]
    odd_y = parity[1]
    dx = (2 * odd_x, 1, 2 - 2 * odd_x)[step_row]
    dy = (2 - 2 * odd_y, 1, 2 * odd_y)[step_col]
    return 3 * dx + dy


def start_kernel(parity, counts, probes, far, near, mask):
    lane = lax.broadcasted_iota(jnp.int32, (1, probes.shape[3]), 1)
    for row, out in enumerate((far, near)):
        for col in range(COLS):
            x, y = place(parity, row, col)
            live = jnp.where(lane < 3 * counts[x, y], 1.0, 0.0)
            mask[row, col] = live
            out[col] = (probes[x, y].astype(jnp.float32) * live).astype(jnp.bfloat16)


AHEAD = 3


def load_kernel(parity, blocks, far, near, out, total, sems):
    cells = [(row, col) for row in range(ROWS) for col in range(COLS)]

    def begin(row, col):
        x, y = place(parity, row, col)
        for step_row in range(3):
            for step_col in range(3):
                pltpu.make_async_copy(
                    blocks.at[x, y, toward(parity, step_row, step_col)],
                    out.at[row, col, 3 * step_row + step_col],
                    sems.at[COLS * row + col],
                ).start()

    for cell in cells[:AHEAD]:
        begin(*cell)
    for number, (row, col) in enumerate(cells):
        if number + AHEAD < len(cells):
            begin(*cells[number + AHEAD])
        pltpu.make_async_copy(blocks.at[row, col], out.at[row, col], sems.at[COLS * row + col]).wait()
        total[row, col] = own_product(far, near, out, row, col)


def product(blocks, row, col, pieces):
    left = jnp.concatenate([blocks[row, col, slot] for slot, _ in pieces], axis=1)
    right = jnp.concatenate([v for _, v in pieces], axis=1)
    return lax.dot_general(left, right, FORWARD, preferred_element_type=jnp.float32)


def own_product(far, near, blocks, row, col):
    pieces = []
    for other, ref in enumerate((far, near)):
        step_row = other - row + 1
        for step_col in range(3):
            c = col + step_col - 1
            if 0 <= c < COLS:
                pieces.append((3 * step_row + step_col, ref[c]))
    return product(blocks, row, col, pieces)


def own_kernel(far, near, blocks, total):
    for row in range(ROWS):
        for col in range(COLS):
            total[row, col] = own_product(far, near, blocks, row, col)


def row_product(ref, blocks, row, col):
    pieces = []
    for step_col in range(3):
        c = col + step_col - 1
        if 0 <= c < COLS:
            pieces.append((3 * (2 * row) + step_col, ref[c]))
    return product(blocks, row, col, pieces)


def column_product(ref, blocks, row, col):
    step_col = 0 if col == 0 else 2
    return product(blocks, row, col, [(3 * s + step_col, ref[row + s]) for s in range(3)])


def edge_kernel(halo_far, far, near, halo_near, core_edge, chip_edge):
    for slot, ref in enumerate((halo_far, far, near, halo_near)):
        core_edge[slot] = ref[0]
        chip_edge[slot] = ref[COLS - 1]


def advance(index, coeffs, mask, state, cols, slot, row, raw):
    col = cols[slot]
    applied = jnp.where(mask[row, col] > 0.0, raw.T, 0.0)
    first = None
    if index in (1, 2, TERMS - 1):
        first = state[-2:][row][col].astype(jnp.float32)
    if index == 1:
        return applied, coeffs[0] * first + coeffs[1] * applied, None
    if index == 2:
        summed, before = state[0][row, slot], first
    else:
        summed, before = state[0][row, slot], state[1][row, slot]
    term = 2.0 * applied - before
    summed = summed + coeffs[index] * term
    msd = None
    if index == TERMS - 1:
        msd = jnp.sum(first * summed, axis=0, keepdims=True) * (1.0 / raw.shape[1])
    return term, summed, msd


def state_size(index):
    return {1: 2, 2: 3, TERMS - 1: 4}.get(index, 2)


def make_rows(index, coeffs):
    def rows(mask, halo_far, halo_near, blocks, partial, *refs):
        state, outs = refs[: state_size(index)], refs[state_size(index) :]
        for row, ref in enumerate((halo_far, halo_near)):
            for col in (1, 2, 0, 3):
                raw = partial[row, col] + row_product(ref, blocks, row, col)
                if col in (0, 3):
                    outs[0 if col == 0 else 1][row] = raw
                    continue
                slot = col - 1
                term, summed, msd = advance(index, coeffs, mask, state, (1, 2), slot, row, raw)
                if index == TERMS - 1:
                    outs[2][row, slot] = summed.astype(jnp.bfloat16)
                    outs[3][row, slot] = msd
                else:
                    outs[2][row, slot] = term.astype(jnp.bfloat16)
                    outs[3][row, slot] = summed
                    if index < TERMS - 2:
                        outs[4][row, slot] = term

    return rows


def make_core(index, coeffs):
    def core(mask, halo, blocks, partial, *refs):
        state, outs = refs[: state_size(index)], refs[state_size(index) :]
        for row in range(ROWS):
            raw = partial[row] + column_product(halo, blocks, row, 0)
            term, summed, msd = advance(index, coeffs, mask, state, (0,), 0, row, raw)
            if index == TERMS - 1:
                outs[0][row, 0] = summed.astype(jnp.bfloat16)
                outs[1][row, 0] = msd
            else:
                outs[0][row, 0] = term.astype(jnp.bfloat16)
                outs[1][row, 0] = summed
                if index < TERMS - 2:
                    outs[2][row, 0] = term

    return core


def make_chip(index, coeffs):
    last = index == TERMS - 1

    def chip(mask, halo, blocks, partial, inner, core, *refs):
        if last:
            parity, inner_msd, core_msd = refs[:3]
            refs = refs[3:]
        state, outs = refs[: state_size(index)], refs[state_size(index) :]
        for row in range(ROWS):
            raw = partial[row] + column_product(halo, blocks, row, 3)
            term, summed, msd = advance(index, coeffs, mask, state, (3,), 0, row, raw)
            if not last:
                message = outs[row]
                message[0] = core[row, 0]
                message[1] = inner[row, 0]
                message[2] = inner[row, 1]
                message[3] = term.astype(jnp.bfloat16)
                outs[2][row, 0] = summed
                if index < TERMS - 2:
                    outs[3][row, 0] = term
                continue
            displacements, msd_out = outs
            pieces = [core[row, 0], inner[row, 0], inner[row, 1], summed.astype(jnp.bfloat16)]
            means = [core_msd[row, 0], inner_msd[row, 0], inner_msd[row, 1], msd]
            for col in range(COLS):
                x, y = place(parity, row, col)
                displacements[x, y] = pieces[col]
            x, _ = place(parity, row, 0)
            msd_out[x] = jnp.where(
                parity[1] == 1, jnp.concatenate(means, axis=0), jnp.concatenate(means[::-1], axis=0)
            )

    return chip


def local(probes, counts, blocks):
    coeffs = chebyshev_weights(TERMS)
    x_index = lax.axis_index("gx")
    y_index = lax.axis_index("gy")
    parity = jnp.stack([x_index % 2, y_index % 2]).astype(jnp.int32)
    vmem = pl.BlockSpec(memory_space=pltpu.VMEM)
    smem = pl.BlockSpec(memory_space=pltpu.SMEM)
    hbm = pl.BlockSpec(memory_space=pl.ANY)
    dofs = probes.shape[3]
    count = probes.shape[2]
    cells = (COLS, count, dofs)
    raw = jax.ShapeDtypeStruct((ROWS, COLS, dofs, count), jnp.float32)
    rounded = jax.ShapeDtypeStruct(cells, jnp.bfloat16)
    params = pltpu.CompilerParams(vmem_limit_bytes=16 * 1024 * 1024)

    def cost(pairs):
        flops = 2 * pairs * count * dofs * dofs * 4
        return pl.CostEstimate(flops=flops, bytes_accessed=pairs * dofs * dofs * 2, transcendentals=0)

    def swap(value, axis, far):
        size = lax.axis_size(axis)
        if far:
            pairs = [(i, (i + 1) % size if i % 2 else (i - 1) % size) for i in range(size)]
        else:
            pairs = [(i, i ^ 1) for i in range(size)]
        return lax.ppermute(value, axis, pairs)

    far, near, mask = pl.pallas_call(
        start_kernel,
        out_shape=(rounded, rounded, jax.ShapeDtypeStruct((ROWS, COLS, 1, dofs), jnp.float32)),
        in_specs=[smem, smem, vmem],
        out_specs=(vmem, vmem, vmem),
        compiler_params=params,
        name="start",
    )(parity, counts, probes)
    start = [far, near]

    def column_state(cols, dtype):
        return jax.ShapeDtypeStruct((ROWS, cols, count, dofs), dtype)

    def run(body, operands, outs, pairs):
        return pl.pallas_call(
            body,
            out_shape=outs,
            in_specs=[smem if operand is parity else vmem for operand in operands],
            out_specs=tuple([vmem] * len(outs)),
            compiler_params=params,
            cost_estimate=cost(pairs),
        )(*operands)

    edge = jax.ShapeDtypeStruct((ROWS, dofs, count), jnp.float32)
    saved = {"inner": [], "core": [], "chip": []}
    held = None
    for index in range(1, TERMS):
        last = index == TERMS - 1
        halo_near = swap(near, "gx", False)
        halo_far = swap(far, "gx", True)
        if index == 1:
            held, partial = pl.pallas_call(
                load_kernel,
                out_shape=(pltpu.VMEM(blocks.shape, blocks.dtype), raw),
                in_specs=[smem, hbm, vmem, vmem],
                out_specs=(vmem, vmem),
                scratch_shapes=[pltpu.SemaphoreType.DMA((ROWS * COLS,))],
                compiler_params=params,
                cost_estimate=pl.CostEstimate(flops=0, bytes_accessed=blocks.size * 4, transcendentals=0),
                name="load",
            )(parity, blocks, far, near)
        else:
            partial = pl.pallas_call(
                own_kernel,
                out_shape=raw,
                in_specs=[vmem, vmem, vmem],
                out_specs=vmem,
                compiler_params=params,
                cost_estimate=cost(40),
                name="own",
            )(far, near, held)
        halo_far, halo_near, partial = lax.optimization_barrier((halo_far, halo_near, partial))
        core_edge, chip_edge = pl.pallas_call(
            edge_kernel,
            out_shape=(rounded, rounded),
            in_specs=[vmem] * 4,
            out_specs=(vmem, vmem),
            compiler_params=params,
            name="edges",
        )(halo_far, far, near, halo_near)
        halo_core = swap(core_edge, "gy", False)
        halo_chip = swap(chip_edge, "gy", True)

        def state(name, index=index, last=last):
            return saved[name] + (start if index <= 2 or last else [])

        def outputs(cols, index=index, last=last):
            if last:
                mean = jax.ShapeDtypeStruct((ROWS, cols, 1, dofs), jnp.float32)
                return (column_state(cols, jnp.bfloat16), mean)
            wide = column_state(cols, jnp.float32)
            return (column_state(cols, jnp.bfloat16),) + (wide,) * (2 if index < TERMS - 2 else 1)

        def keep(name, summed, term=None, index=index):
            terms[name].append(term)
            saved[name] = [summed] + ([terms[name][-2]] if index >= 2 else [])

        if index == 1:
            terms = {"inner": [], "core": [], "chip": []}
        fixed = [mask]
        core_raw, chip_raw, inner, *rest = run(
            make_rows(index, coeffs),
            fixed + [halo_far, halo_near, held, partial] + state("inner"),
            (edge, edge) + outputs(2),
            20,
        )
        core, *core_rest = run(
            make_core(index, coeffs),
            fixed + [halo_core, held, core_raw] + state("core"),
            outputs(1),
            6,
        )
        operands = fixed + [halo_chip, held, chip_raw, inner, core]
        if last:
            operands += [parity, rest[0], core_rest[0]]
            outs = (
                jax.ShapeDtypeStruct(probes.shape, jnp.bfloat16),
                jax.ShapeDtypeStruct((ROWS, COLS, dofs), jnp.float32),
            )
        else:
            wide = column_state(1, jnp.float32)
            outs = (rounded, rounded) + (wide,) * (2 if index < TERMS - 2 else 1)
        results = run(make_chip(index, coeffs), operands + state("chip"), outs, 6)
        if not last:
            far, near = results[:2]
            keep("inner", *rest)
            keep("core", *core_rest)
            keep("chip", *results[2:])
    return tuple(results)


def solution(mesh):
    return jax.shard_map(
        local,
        mesh=mesh,
        in_specs=(P("gx", "gy", None, None), P("gx", "gy"), P("gx", "gy", None, None, None)),
        out_specs=(P("gx", "gy", None, None), P("gx", "gy", None)),
        check_vma=False,
    )
```

```python
import math

import jax
import jax.numpy as jnp
import numpy as np
from jax import lax
from jax.experimental import pallas as pl
from jax.experimental.pallas import tpu as pltpu
from jax.sharding import PartitionSpec as P


TERMS = 8


inverse_temp = 4.0
low_band = 0.02
high_band = 1.0

ROWS = 2
COLS = 4
FORWARD = (((1,), (1,)), ((), ()))


def chebyshev_weights(term_count):
    node_count = 64
    values = []
    angles = []
    for n in range(node_count):
        angle = math.pi * (n + 0.5) / node_count
        energy = low_band + (math.cos(angle) + 1.0) * (high_band - low_band) / 2.0
        root_energy = math.sqrt(energy)
        decay = math.exp(-inverse_temp * root_energy)
        values.append((1.0 + decay) / (1.0 - decay) / (2.0 * root_energy))
        angles.append(angle)
    coeffs = []
    for k in range(term_count):
        total = 0.0
        for n in range(node_count):
            total = total + values[n] * math.cos(k * angles[n])
        coeffs.append(2.0 / node_count * total)
    coeffs[0] = coeffs[0] / 2.0
    return [float(np.float32(c)) for c in coeffs]


def place(parity, row, col):
    odd_x = parity[0]
    odd_y = parity[1]
    x = odd_x if row == 0 else 1 - odd_x
    y = (3 - col) + odd_y * (2 * col - 3)
    return x, y


def toward(parity, step_row, step_col):
    odd_x = parity[0]
    odd_y = parity[1]
    dx = (2 * odd_x, 1, 2 - 2 * odd_x)[step_row]
    dy = (2 - 2 * odd_y, 1, 2 * odd_y)[step_col]
    return 3 * dx + dy


def start_kernel(parity, counts, probes, far, near, mask):
    lane = lax.broadcasted_iota(jnp.int32, (1, probes.shape[3]), 1)
    for row, out in enumerate((far, near)):
        for col in range(COLS):
            x, y = place(parity, row, col)
            live = jnp.where(lane < 3 * counts[x, y], 1.0, 0.0)
            mask[row, col] = live
            out[col] = (probes[x, y].astype(jnp.float32) * live).astype(jnp.bfloat16)


AHEAD = 3


def load_kernel(parity, blocks, far, near, out, total, sems):
    cells = [(row, col) for row in range(ROWS) for col in range(COLS)]

    def begin(row, col):
        x, y = place(parity, row, col)
        for step_row in range(3):
            for step_col in range(3):
                pltpu.make_async_copy(
                    blocks.at[x, y, toward(parity, step_row, step_col)],
                    out.at[row, col, 3 * step_row + step_col],
                    sems.at[COLS * row + col],
                ).start()

    for cell in cells[:AHEAD]:
        begin(*cell)
    for number, (row, col) in enumerate(cells):
        if number + AHEAD < len(cells):
            begin(*cells[number + AHEAD])
        pltpu.make_async_copy(blocks.at[row, col], out.at[row, col], sems.at[COLS * row + col]).wait()
        total[row, col] = own_product(far, near, out, row, col)


def product(blocks, row, col, pieces):
    left = jnp.concatenate([blocks[row, col, slot] for slot, _ in pieces], axis=1)
    right = jnp.concatenate([v for _, v in pieces], axis=1)
    return lax.dot_general(left, right, FORWARD, preferred_element_type=jnp.float32)


def own_product(far, near, blocks, row, col):
    pieces = []
    for other, ref in enumerate((far, near)):
        step_row = other - row + 1
        for step_col in range(3):
            c = col + step_col - 1
            if 0 <= c < COLS:
                pieces.append((3 * step_row + step_col, ref[c]))
    return product(blocks, row, col, pieces)


def own_kernel(far, near, blocks, total):
    for row in range(ROWS):
        for col in range(COLS):
            total[row, col] = own_product(far, near, blocks, row, col)


def near_kernel(halo_near, blocks, partial, total):
    for col in range(COLS):
        total[1, col] = partial[1, col] + row_product(halo_near, blocks, 1, col)
    total[0] = partial[0]


def row_product(ref, blocks, row, col):
    pieces = []
    for step_col in range(3):
        c = col + step_col - 1
        if 0 <= c < COLS:
            pieces.append((3 * (2 * row) + step_col, ref[c]))
    return product(blocks, row, col, pieces)


def column_product(ref, blocks, row, col):
    step_col = 0 if col == 0 else 2
    return product(blocks, row, col, [(3 * s + step_col, ref[row + s]) for s in range(3)])


def edge_kernel(halo_far, far, near, halo_near, core_edge, chip_edge):
    for slot, ref in enumerate((halo_far, far, near, halo_near)):
        core_edge[slot] = ref[0]
        chip_edge[slot] = ref[COLS - 1]


def advance(index, coeffs, mask, state, cols, slot, row, raw):
    col = cols[slot]
    applied = jnp.where(mask[row, col] > 0.0, raw.T, 0.0)
    first = None
    if index in (1, 2, TERMS - 1):
        first = state[-2:][row][col].astype(jnp.float32)
    if index == 1:
        return applied, coeffs[0] * first + coeffs[1] * applied, None
    if index == 2:
        summed, before = state[0][row, slot], first
    else:
        summed, before = state[0][row, slot], state[1][row, slot]
    term = 2.0 * applied - before
    summed = summed + coeffs[index] * term
    msd = None
    if index == TERMS - 1:
        msd = jnp.sum(first * summed, axis=0, keepdims=True) * (1.0 / raw.shape[1])
    return term, summed, msd


def state_size(index):
    return {1: 2, 2: 3, TERMS - 1: 4}.get(index, 2)


def make_rows(index, coeffs):
    def rows(mask, halo_far, blocks, partial, *refs):
        state, outs = refs[: state_size(index)], refs[state_size(index) :]
        for row in range(ROWS):
            for col in (1, 2, 0, 3):
                raw = partial[row, col]
                if row == 0:
                    raw = raw + row_product(halo_far, blocks, row, col)
                if col in (0, 3):
                    outs[0 if col == 0 else 1][row] = raw
                    continue
                slot = col - 1
                term, summed, msd = advance(index, coeffs, mask, state, (1, 2), slot, row, raw)
                if index == TERMS - 1:
                    outs[2][row, slot] = summed.astype(jnp.bfloat16)
                    outs[3][row, slot] = msd
                else:
                    outs[2][row, slot] = term.astype(jnp.bfloat16)
                    outs[3][row, slot] = summed
                    if index < TERMS - 2:
                        outs[4][row, slot] = term

    return rows


def make_core(index, coeffs):
    def core(mask, halo, blocks, partial, *refs):
        state, outs = refs[: state_size(index)], refs[state_size(index) :]
        for row in range(ROWS):
            raw = partial[row] + column_product(halo, blocks, row, 0)
            term, summed, msd = advance(index, coeffs, mask, state, (0,), 0, row, raw)
            if index == TERMS - 1:
                outs[0][row, 0] = summed.astype(jnp.bfloat16)
                outs[1][row, 0] = msd
            else:
                outs[0][row, 0] = term.astype(jnp.bfloat16)
                outs[1][row, 0] = summed
                if index < TERMS - 2:
                    outs[2][row, 0] = term

    return core


def make_chip(index, coeffs):
    last = index == TERMS - 1

    def chip(mask, halo, blocks, partial, inner, core, *refs):
        if last:
            parity, inner_msd, core_msd = refs[:3]
            refs = refs[3:]
        state, outs = refs[: state_size(index)], refs[state_size(index) :]
        for row in range(ROWS):
            raw = partial[row] + column_product(halo, blocks, row, 3)
            term, summed, msd = advance(index, coeffs, mask, state, (3,), 0, row, raw)
            if not last:
                message = outs[row]
                message[0] = core[row, 0]
                message[1] = inner[row, 0]
                message[2] = inner[row, 1]
                message[3] = term.astype(jnp.bfloat16)
                outs[2][row, 0] = summed
                if index < TERMS - 2:
                    outs[3][row, 0] = term
                continue
            displacements, msd_out = outs
            pieces = [core[row, 0], inner[row, 0], inner[row, 1], summed.astype(jnp.bfloat16)]
            means = [core_msd[row, 0], inner_msd[row, 0], inner_msd[row, 1], msd]
            for col in range(COLS):
                x, y = place(parity, row, col)
                displacements[x, y] = pieces[col]
            x, _ = place(parity, row, 0)
            msd_out[x] = jnp.where(
                parity[1] == 1, jnp.concatenate(means, axis=0), jnp.concatenate(means[::-1], axis=0)
            )

    return chip


def local(probes, counts, blocks):
    coeffs = chebyshev_weights(TERMS)
    x_index = lax.axis_index("gx")
    y_index = lax.axis_index("gy")
    parity = jnp.stack([x_index % 2, y_index % 2]).astype(jnp.int32)
    vmem = pl.BlockSpec(memory_space=pltpu.VMEM)
    smem = pl.BlockSpec(memory_space=pltpu.SMEM)
    hbm = pl.BlockSpec(memory_space=pl.ANY)
    dofs = probes.shape[3]
    count = probes.shape[2]
    cells = (COLS, count, dofs)
    raw = jax.ShapeDtypeStruct((ROWS, COLS, dofs, count), jnp.float32)
    rounded = jax.ShapeDtypeStruct(cells, jnp.bfloat16)
    params = pltpu.CompilerParams(vmem_limit_bytes=16 * 1024 * 1024)

    def cost(pairs):
        flops = 2 * pairs * count * dofs * dofs * 4
        return pl.CostEstimate(flops=flops, bytes_accessed=pairs * dofs * dofs * 2, transcendentals=0)

    def swap(value, axis, far):
        size = lax.axis_size(axis)
        if far:
            pairs = [(i, (i + 1) % size if i % 2 else (i - 1) % size) for i in range(size)]
        else:
            pairs = [(i, i ^ 1) for i in range(size)]
        return lax.ppermute(value, axis, pairs)

    far, near, mask = pl.pallas_call(
        start_kernel,
        out_shape=(rounded, rounded, jax.ShapeDtypeStruct((ROWS, COLS, 1, dofs), jnp.float32)),
        in_specs=[smem, smem, vmem],
        out_specs=(vmem, vmem, vmem),
        compiler_params=params,
        name="start",
    )(parity, counts, probes)
    start = [far, near]

    def column_state(cols, dtype):
        return jax.ShapeDtypeStruct((ROWS, cols, count, dofs), dtype)

    def run(body, operands, outs, pairs):
        return pl.pallas_call(
            body,
            out_shape=outs,
            in_specs=[smem if operand is parity else vmem for operand in operands],
            out_specs=tuple([vmem] * len(outs)),
            compiler_params=params,
            cost_estimate=cost(pairs),
        )(*operands)

    edge = jax.ShapeDtypeStruct((ROWS, dofs, count), jnp.float32)
    saved = {"inner": [], "core": [], "chip": []}
    held = None
    for index in range(1, TERMS):
        last = index == TERMS - 1
        halo_near = swap(near, "gx", False)
        halo_far = swap(far, "gx", True)
        if index == 1:
            held, partial = pl.pallas_call(
                load_kernel,
                out_shape=(pltpu.VMEM(blocks.shape, blocks.dtype), raw),
                in_specs=[smem, hbm, vmem, vmem],
                out_specs=(vmem, vmem),
                scratch_shapes=[pltpu.SemaphoreType.DMA((ROWS * COLS,))],
                compiler_params=params,
                cost_estimate=pl.CostEstimate(flops=0, bytes_accessed=blocks.size * 4, transcendentals=0),
                name="load",
            )(parity, blocks, far, near)
        else:
            partial = pl.pallas_call(
                own_kernel,
                out_shape=raw,
                in_specs=[vmem, vmem, vmem],
                out_specs=vmem,
                compiler_params=params,
                cost_estimate=cost(40),
                name="own",
            )(far, near, held)
        halo_near, partial = lax.optimization_barrier((halo_near, partial))
        partial = pl.pallas_call(
            near_kernel,
            out_shape=raw,
            in_specs=[vmem] * 3,
            out_specs=vmem,
            input_output_aliases={2: 0},
            compiler_params=params,
            cost_estimate=cost(10),
            name="near",
        )(halo_near, held, partial)
        halo_far, partial = lax.optimization_barrier((halo_far, partial))
        core_edge, chip_edge = pl.pallas_call(
            edge_kernel,
            out_shape=(rounded, rounded),
            in_specs=[vmem] * 4,
            out_specs=(vmem, vmem),
            compiler_params=params,
            name="edges",
        )(halo_far, far, near, halo_near)
        halo_core = swap(core_edge, "gy", False)
        halo_chip = swap(chip_edge, "gy", True)

        def state(name, index=index, last=last):
            return saved[name] + (start if index <= 2 or last else [])

        def outputs(cols, index=index, last=last):
            if last:
                mean = jax.ShapeDtypeStruct((ROWS, cols, 1, dofs), jnp.float32)
                return (column_state(cols, jnp.bfloat16), mean)
            wide = column_state(cols, jnp.float32)
            return (column_state(cols, jnp.bfloat16),) + (wide,) * (2 if index < TERMS - 2 else 1)

        def keep(name, summed, term=None, index=index):
            terms[name].append(term)
            saved[name] = [summed] + ([terms[name][-2]] if index >= 2 else [])

        if index == 1:
            terms = {"inner": [], "core": [], "chip": []}
        fixed = [mask]
        core_raw, chip_raw, inner, *rest = run(
            make_rows(index, coeffs),
            fixed + [halo_far, held, partial] + state("inner"),
            (edge, edge) + outputs(2),
            20,
        )
        core, *core_rest = run(
            make_core(index, coeffs),
            fixed + [halo_core, held, core_raw] + state("core"),
            outputs(1),
            6,
        )
        operands = fixed + [halo_chip, held, chip_raw, inner, core]
        if last:
            operands += [parity, rest[0], core_rest[0]]
            outs = (
                jax.ShapeDtypeStruct(probes.shape, jnp.bfloat16),
                jax.ShapeDtypeStruct((ROWS, COLS, dofs), jnp.float32),
            )
        else:
            wide = column_state(1, jnp.float32)
            outs = (rounded, rounded) + (wide,) * (2 if index < TERMS - 2 else 1)
        results = run(make_chip(index, coeffs), operands + state("chip"), outs, 6)
        if not last:
            far, near = results[:2]
            keep("inner", *rest)
            keep("core", *core_rest)
            keep("chip", *results[2:])
    return tuple(results)


def solution(mesh):
    return jax.shard_map(
        local,
        mesh=mesh,
        in_specs=(P("gx", "gy", None, None), P("gx", "gy"), P("gx", "gy", None, None, None)),
        out_specs=(P("gx", "gy", None, None), P("gx", "gy", None)),
        check_vma=False,
    )
```
